32 devices in a mesh: wide: 4 (over x, core), sixteen: 8 (over z, y).
Axes of the slice: x: 2, y: 2, z: 4, core: 2. Of those that a mesh axis runs over, the one named last changes fastest.
Arguments:
- features: float32 [4, 8, 512, 128], P('wide', 'sixteen'), may hold values from -6 to 6
- positions: float32 [4, 8, 3, 512], P('wide', 'sixteen'), may hold values from 0 to 1, as said below
- tile_lists: int32 [4, 8, 4, 16], P('wide', 'sixteen'), may hold values from 0 to 36, as said below
- value_proj: float32 [128, 128], replicated, may hold values from -0.5 to 0.5
- radial_mix: float32 [16, 128], replicated, may hold values from -1.5 to 1.5
- charge_proj: float32 [128, 128], replicated, may hold values from -0.5 to 0.5
- screening: float32 [128], P(('wide', 'sixteen')), may hold values from 20 to 200
- smearing: float32 [128], P(('wide', 'sixteen')), may hold values from 0.003 to 0.02
- mesh_gain: float32 [128], replicated, may hold values from 0.25 to 1.75
- mesh_up: float32 [128, 256], replicated, may hold values from -0.5 to 0.5
- mesh_down: float32 [256, 128], replicated, may hold values from -0.375 to 0.375
- long_proj: float32 [128, 128], replicated, may hold values from -0.5 to 0.5
- atom_gain: float32 [128], replicated, may hold values from 0.25 to 1.75
- atom_up: float32 [128, 256], replicated, may hold values from -0.5 to 0.5
- atom_down: float32 [256, 128], replicated, may hold values from -0.375 to 0.375
Outputs:
- updated: float32 [4, 8, 512, 128], P('wide', 'sixteen')
The draws below stay inside these ranges and needn't reach their ends.
Inputs may be any that keep to these rules, and one draw needn't show every extreme that they name: `tile_lists`: each list of tile t of a block holds codes nb * 4 + t2 of tiles of the 3 x 3 blocks around it with (t2 - t) mod 4 equal to 0, 1 or 3; its first entry is the tile itself, 16 + t; its live entries are distinct; empty entries hold 36 and stand after all live ones; every list has 1 to 16 live entries and some list has 16. `positions`: the third coordinate of atom a of a block lies between a / 512 and (a + 1) / 512.
All inputs are finite; a program needn't handle non-finite values.
Results may differ from the reference program's by a relative error of at most 0.0003.
Values sent between devices are 32-bit elements; how exact they have to be, the bound alone decides.
A program may use at most 128 MiB of HBM per device.

```python
import math
import jax
import jax.numpy as jnp
from jax import lax

F = 128
C = 128
NB = 16
MESH = 64
HM = 256
FH = 256
TILE = 128
K = 16
ATOM_DEV = 512
BLOCKS_W = 4
BLOCKS_S = 8
N_WIDE = 4
N_SIXTEEN = 8


def draw_positions(key, part):
    key_plane = jax.random.fold_in(key, 21)
    key_depth = jax.random.fold_in(key, 22)
    plane = jax.random.uniform(key_plane, (BLOCKS_W, BLOCKS_S, 2, ATOM_DEV), jnp.float32)
    jitter = jax.random.uniform(key_depth, (BLOCKS_W, BLOCKS_S, 1, ATOM_DEV), jnp.float32)
    ranks = jnp.arange(ATOM_DEV).astype(jnp.float32)
    depth = (ranks[None, None, None, :] + jitter) / ATOM_DEV
    depth = jnp.minimum(depth, 1.0)
    return jnp.concatenate([plane, depth], axis=2).astype(jnp.float32)


def draw_tile_lists(key, part):
    tiles_per = ATOM_DEV // TILE
    empty_code = 9 * tiles_per
    blocks = BLOCKS_W * BLOCKS_S
    key_busy = jax.random.fold_in(key, 11)
    key_count = jax.random.fold_in(key, 12)
    key_score = jax.random.fold_in(key, 13)
    busy_level = jax.random.randint(key_busy, (blocks, 1), 0, 4)
    counts = 1 + jax.random.randint(key_count, (blocks, tiles_per), 0, K) // (1 + busy_level)
    counts = counts.at[0, 0].set(K)
    code_range = jnp.arange(empty_code, dtype=jnp.int32)
    code_tile = code_range % tiles_per
    own_tile = jnp.arange(tiles_per, dtype=jnp.int32)
    gap = (code_tile[None, :] - own_tile[:, None]) % tiles_per
    is_near = (gap == 0) | (gap == 1) | (gap == tiles_per - 1)
    scores = jax.random.randint(key_score, (blocks, tiles_per, empty_code), 0, 65536) * empty_code + code_range
    own_codes = 4 * tiles_per + own_tile
    is_own = code_range[None, None, :] == own_codes[None, :, None]
    scores = jnp.where(is_near[None] & ~is_own, scores, -1)
    picked = lax.top_k(scores, K - 1)[1].astype(jnp.int32)
    first_codes = jnp.broadcast_to(own_codes[None, :, None], (blocks, tiles_per, 1))
    tile_codes = jnp.concatenate([first_codes, picked], axis=2)
    slot_index = jnp.arange(K, dtype=jnp.int32)
    tile_codes = jnp.where(slot_index[None, None, :] < counts[:, :, None], tile_codes, empty_code)
    return tile_codes.reshape(BLOCKS_W, BLOCKS_S, tiles_per, K).astype(jnp.int32)


def block_levels(key, dims, split, low, top_value):
    loudness = 1.0
    for axis_at, shards_of in split:
        steps = jax.random.uniform(jax.random.fold_in(jax.random.fold_in(key, 6), axis_at), (shards_of,), jnp.float32, low / len(split), top_value / len(split))
        loudness = loudness * jnp.repeat(jnp.exp(steps), dims[axis_at] // shards_of).reshape((-1,) + (1,) * (len(dims) - 1 - axis_at))
    return loudness


def bell_draw(own_key, extent, scale, reach, split=(), kind=jnp.bfloat16):
    array = jax.random.normal(own_key, extent, jnp.float32) * scale
    if len(split) > 0:
        array = block_levels(own_key, extent, split, -0.22, 0.18) * array
    return jnp.clip(array, min=-reach, max=reach).astype(kind)


def setup_inputs(seed: int = 0) -> dict:
    splits = jax.random.split(jax.random.key(seed), 16)
    return {
        "features": bell_draw(splits[0], (BLOCKS_W, BLOCKS_S, ATOM_DEV, F), 1.0, 6.0, ((0, 4), (1, 8)), jnp.float32),
        "positions": draw_positions(jax.random.fold_in(splits[15], 71), 0),
        "tile_lists": draw_tile_lists(jax.random.fold_in(splits[15], 71), 0),
        "value_proj": bell_draw(splits[3], (F, F), F ** -0.5, 0.5, (), jnp.float32),
        "radial_mix": bell_draw(splits[4], (NB, F), NB ** -0.5, 1.5, (), jnp.float32),
        "charge_proj": bell_draw(splits[5], (F, C), F ** -0.5, 0.5, (), jnp.float32),
        "screening": jnp.clip(jnp.exp(math.log(200.0) - 2.3025851 * jax.random.uniform(splits[6], (C,), jnp.float32) ** block_levels(splits[6], (C,), ((0, 32),), -0.2, 0.2)), 20.0, 200.0),
        "smearing": jnp.clip(jnp.exp(math.log(0.02) - 1.89712 * jax.random.uniform(splits[7], (C,), jnp.float32) ** block_levels(splits[7], (C,), ((0, 32),), -0.2, 0.2)), 0.003, 0.02),
        "mesh_gain": jnp.clip(1.0 + 0.15 * jax.random.normal(splits[8], (C,), jnp.float32), 0.25, 1.75),
        "mesh_up": bell_draw(splits[9], (C, HM), C ** -0.5, 0.5, (), jnp.float32),
        "mesh_down": bell_draw(splits[10], (HM, C), HM ** -0.5, 0.375, (), jnp.float32),
        "long_proj": bell_draw(splits[11], (C, F), C ** -0.5, 0.5, (), jnp.float32),
        "atom_gain": jnp.clip(1.0 + 0.15 * jax.random.normal(splits[12], (F,), jnp.float32), 0.25, 1.75),
        "atom_up": bell_draw(splits[13], (F, FH), F ** -0.5, 0.5, (), jnp.float32),
        "atom_down": bell_draw(splits[14], (FH, F), FH ** -0.5, 0.375, (), jnp.float32),
    }


exact = lax.Precision.HIGHEST

def short_range(near_values, near_positions, tile_codes, radial_mix, wide_count, sixteen_count):
    atom_count = near_values.shape[2]
    feature_width = near_values.shape[3]
    tiles_per = atom_count // TILE
    basis_count = radial_mix.shape[0]
    empty_code = 9 * tiles_per
    cutoff = 0.8 / max(wide_count, sixteen_count)
    sharpness = 0.5 * (basis_count - 1) ** 2
    centres = jnp.arange(basis_count).astype(jnp.float32) / (basis_count - 1)
    offsets = jnp.arange(3).astype(jnp.float32) - 1.0
    global_x = (near_positions[:, :, 0, :] + offsets[:, None, None]) / wide_count
    global_y = (near_positions[:, :, 1, :] + offsets[None, :, None]) / sixteen_count
    global_z = near_positions[:, :, 2, :]
    placed = jnp.stack([global_x, global_y, global_z], axis=2)
    source_pos = placed.reshape(9, 3, tiles_per, TILE).transpose(0, 2, 1, 3).reshape(empty_code, 3, TILE)
    source_val = near_values.reshape(empty_code, TILE, feature_width)
    own_pos = source_pos[4 * tiles_per:5 * tiles_per]
    own_codes = 4 * tiles_per + jnp.arange(tiles_per, dtype=jnp.int32)
    diagonal = jnp.eye(TILE, dtype=bool)

    def one_slot(slot_index, running):
        slot_codes = tile_codes[:, slot_index]
        is_live = slot_codes < empty_code
        chosen = jnp.minimum(slot_codes, empty_code - 1)
        other_pos = source_pos[chosen]
        other_val = source_val[chosen]
        offset_vec = other_pos[:, :, None, :] - own_pos[:, :, :, None]
        delta_z = offset_vec[:, 2] - jnp.floor(offset_vec[:, 2] + 0.5)
        radius = jnp.sqrt(offset_vec[:, 0] ** 2 + offset_vec[:, 1] ** 2 + delta_z ** 2) / cutoff
        envelope = jnp.where(radius < 1.0, 0.5 * (jnp.cos(jnp.pi * radius) + 1.0), 0.0)
        itself = (slot_codes == own_codes)[:, None, None] & diagonal[None]
        envelope = jnp.where(is_live[:, None, None] & ~itself, envelope, 0.0)
        basis_vals = jnp.exp(-sharpness * (radius[:, None] - centres[None, :, None, None]) ** 2) * envelope[:, None]
        partial_sum = jnp.einsum('tbij,tjc->tbic', basis_vals, other_val, precision=exact)
        return running + jnp.einsum('tbic,bc->tic', partial_sum, radial_mix, precision=exact)
    running = lax.fori_loop(0, tile_codes.shape[1], one_slot, jnp.zeros((tiles_per, TILE, feature_width), jnp.float32))
    return running.reshape(atom_count, feature_width)

def stencil(coords):
    floored = jnp.floor(coords)
    fraction = coords - floored
    base_cell = floored.astype(jnp.int32)
    cell_list = []
    weights = []
    for corner in range(8):
        corner_steps = (corner // 4, corner // 2 % 2, corner % 2)
        cell_index = jnp.zeros(coords.shape[1], jnp.int32)
        weight = jnp.ones(coords.shape[1], jnp.float32)
        for dimension in range(3):
            cell_index = cell_index * MESH + (base_cell[dimension] + corner_steps[dimension]) % MESH
            if corner_steps[dimension]:
                weight = weight * fraction[dimension]
            else:
                weight = weight * (1.0 - fraction[dimension])
        cell_list.append(cell_index)
        weights.append(weight)
    return (cell_list, weights)

def filter_kernel(screening, smearing):
    sample_index = jnp.arange(MESH, dtype=jnp.int32)
    signed = jnp.where(sample_index < MESH // 2, sample_index, sample_index - MESH).astype(jnp.float32)
    wavenumber = 2.0 * jnp.pi * signed
    squares = wavenumber[:, None, None] ** 2 + wavenumber[None, :, None] ** 2 + wavenumber[None, None, :] ** 2
    kappa_sq = screening[:, None, None, None] ** 2
    return kappa_sq * jnp.exp(-0.5 * squares[None] * smearing[:, None, None, None] ** 2) / (squares[None] + kappa_sq)

def mesh_mlp(by_cells, mesh_gain, mesh_up, mesh_down):
    inverse_rms = lax.rsqrt(lax.optimization_barrier(jnp.mean(by_cells ** 2, axis=0, keepdims=True)) + 1e-06)
    normed = by_cells * inverse_rms * mesh_gain[:, None]
    hidden = jax.nn.silu(jnp.einsum('ch,cn->hn', mesh_up, normed, precision=exact))
    return jnp.einsum('hc,hn->cn', mesh_down, hidden, precision=exact)

def reference(features, positions, tile_lists, value_proj, radial_mix, charge_proj, screening, smearing, mesh_gain, mesh_up, mesh_down, long_proj, atom_gain, atom_up, atom_down):
    wide_count = N_WIDE
    sixteen_count = N_SIXTEEN
    devices = wide_count * sixteen_count
    atom_count = features.shape[2]
    feature_width = features.shape[3]
    channels = charge_proj.shape[1]
    cells_total = MESH ** 3
    values = jnp.einsum('xyaf,fg->xyag', features, value_proj, precision=exact)

    def one_block(block_index):
        row_index = block_index // sixteen_count
        column = block_index % sixteen_count
        row_list = (row_index + jnp.arange(3, dtype=jnp.int32) - 1) % wide_count
        column_list = (column + jnp.arange(3, dtype=jnp.int32) - 1) % sixteen_count
        near_values = values[row_list][:, column_list]
        near_positions = positions[row_list][:, column_list]
        return short_range(near_values, near_positions, tile_lists[row_index, column], radial_mix, wide_count, sixteen_count)
    messages = lax.map(one_block, jnp.arange(devices, dtype=jnp.int32)).reshape(devices * atom_count, feature_width)
    flat_features = features.reshape(devices * atom_count, feature_width)
    charges = jnp.dot(flat_features, charge_proj, precision=exact)
    block_x = jnp.arange(wide_count).astype(jnp.float32)
    block_y = jnp.arange(sixteen_count).astype(jnp.float32)
    coords_x = ((block_x[:, None, None] + positions[:, :, 0, :]) * (MESH / wide_count)).reshape(-1)
    coords_y = ((block_y[None, :, None] + positions[:, :, 1, :]) * (MESH / sixteen_count)).reshape(-1)
    coords_z = (positions[:, :, 2, :] * MESH).reshape(-1)
    cell_list, weights = stencil(jnp.stack([coords_x, coords_y, coords_z]))
    density = jnp.zeros((cells_total, channels), jnp.float32)
    for corner in range(8):
        density = density.at[cell_list[corner]].add(weights[corner][:, None] * charges)
    field_all = density.T.reshape(channels, MESH, MESH, MESH)

    def smooth(channel_item):
        field_grid, kappa_value, sigma_value = channel_item
        kernel = filter_kernel(kappa_value[None], sigma_value[None])[0]
        return jnp.real(jnp.fft.ifftn(jnp.fft.fftn(field_grid) * kernel))
    potential = lax.map(smooth, (field_all, screening, smearing)).reshape(channels, cells_total)
    blocks_view = potential.reshape(channels, devices, cells_total // devices).transpose(1, 0, 2)
    mesh_out = lax.map(lambda block_view: mesh_mlp(block_view, mesh_gain, mesh_up, mesh_down), blocks_view)
    mesh_out = mesh_out.transpose(1, 0, 2).reshape(channels, cells_total)
    at_atoms = jnp.zeros((channels, devices * atom_count), jnp.float32)
    for corner in range(8):
        at_atoms = at_atoms + weights[corner][None, :] * mesh_out[:, cell_list[corner]]
    long_terms = jnp.einsum('cn,cf->nf', at_atoms, long_proj, precision=exact)
    summed = flat_features + messages + long_terms
    inverse_rms = lax.rsqrt(lax.optimization_barrier(jnp.mean(summed ** 2, axis=-1, keepdims=True)) + 1e-06)
    normed = summed * inverse_rms * atom_gain
    hidden = jax.nn.silu(jnp.dot(normed, atom_up, precision=exact))
    updated = summed + jnp.dot(hidden, atom_down, precision=exact)
    return updated.reshape(wide_count, sixteen_count, atom_count, feature_width)
```

```python
import jax
import jax.numpy as jnp
from jax import lax
from jax.sharding import PartitionSpec as P

MESH = 64
TILE = 128


fine = lax.Precision.HIGH


def extended_2(block, sides, width):
    for axis, dim in sides:
        count = lax.axis_size(axis)
        forward = [(i, i + 1) for i in range(count - 1)]
        forward.append((count - 1, 0))
        backward = [(target, source) for source, target in forward]
        low = lax.ppermute(
            lax.slice_in_dim(block, block.shape[dim] - width, None, axis=dim), axis, forward
        )
        high = lax.ppermute(lax.slice_in_dim(block, 0, width, axis=dim), axis, backward)
        block = jnp.concatenate([low, block, high], axis=dim)
    return block


def passed_along(array, axis, by):
    count = lax.axis_size(axis)
    return lax.ppermute(array, axis, [(i, (i + by) % count) for i in range(count)])


def short_range(near_values, near_positions, tile_codes, radial_mix, wide_count, sixteen_count):
    atom_count = near_values.shape[2]
    feature_width = near_values.shape[3]
    tiles_per = atom_count // TILE
    basis_count = radial_mix.shape[0]
    empty_code = 9 * tiles_per
    cutoff = 0.8 / max(wide_count, sixteen_count)
    sharpness = 0.5 * (basis_count - 1) ** 2
    centres = jnp.arange(basis_count).astype(jnp.float32) / (basis_count - 1)
    offsets = jnp.arange(3).astype(jnp.float32) - 1.0
    global_x = (near_positions[:, :, 0, :] + offsets[:, None, None]) / wide_count
    global_y = (near_positions[:, :, 1, :] + offsets[None, :, None]) / sixteen_count
    global_z = near_positions[:, :, 2, :]
    placed = jnp.stack([global_x, global_y, global_z], axis=2)
    source_pos = (
        placed.reshape(9, 3, tiles_per, TILE).transpose(0, 2, 1, 3).reshape(empty_code, 3, TILE)
    )
    source_val = near_values.reshape(empty_code, TILE, feature_width)
    own_pos = source_pos[4 * tiles_per : 5 * tiles_per]
    own_codes = 4 * tiles_per + jnp.arange(tiles_per, dtype=jnp.int32)
    diagonal = jnp.eye(TILE, dtype=bool)

    def one_slot(slot_index, running):
        slot_codes = tile_codes[:, slot_index]
        is_live = slot_codes < empty_code
        chosen = jnp.minimum(slot_codes, empty_code - 1)
        other_pos = source_pos[chosen]
        other_val = source_val[chosen]
        offset_vec = other_pos[:, :, None, :] - own_pos[:, :, :, None]
        delta_z = offset_vec[:, 2] - jnp.floor(offset_vec[:, 2] + 0.5)
        radius = jnp.sqrt(offset_vec[:, 0] ** 2 + offset_vec[:, 1] ** 2 + delta_z**2) / cutoff
        envelope = jnp.where(radius < 1.0, 0.5 * (jnp.cos(jnp.pi * radius) + 1.0), 0.0)
        itself = (slot_codes == own_codes)[:, None, None] & diagonal[None]
        envelope = jnp.where(is_live[:, None, None] & ~itself, envelope, 0.0)
        basis_vals = (
            jnp.exp(-sharpness * (radius[:, :, None] - centres[None, None, :, None]) ** 2)
            * envelope[:, :, None]
        )
        mixed = other_val[:, None] * radial_mix[None, :, None, :]
        return running + jnp.einsum(
            "tik,tkc->tic",
            basis_vals.reshape(tiles_per, TILE, basis_count * TILE),
            mixed.reshape(tiles_per, basis_count * TILE, feature_width),
            precision=fine,
        )

    live_slots = jnp.max(jnp.sum((tile_codes < empty_code).astype(jnp.int32), axis=1))
    running = lax.fori_loop(
        0, live_slots, one_slot, jnp.zeros((tiles_per, TILE, feature_width), jnp.float32)
    )
    return running.reshape(atom_count, feature_width)


def hat(coords, count):
    return jnp.maximum(
        1.0 - jnp.abs(coords[..., None] - jnp.arange(count).astype(jnp.float32)), 0.0
    )


def plane_weights(pos, step_x, step_y, slab_x, slab_y, count_x, count_y):
    atoms = pos.shape[1]
    per_plane = atoms // MESH
    plane = (jnp.arange(atoms, dtype=jnp.int32) // per_plane).astype(jnp.float32)
    upper = pos[2] * MESH - plane
    flat = (
        hat((pos[0] + step_x) * slab_x, count_x)[:, :, None]
        * hat((pos[1] + step_y) * slab_y, count_y)[:, None, :]
    ).reshape(MESH, per_plane, count_x * count_y)
    upper = upper.reshape(MESH, per_plane, 1)
    return jnp.concatenate([flat * (1.0 - upper), jnp.roll(flat * upper, 1, axis=0)], axis=1)


def filter_kernel(screening, smearing):
    sample_index = jnp.arange(MESH, dtype=jnp.int32)
    signed = jnp.where(sample_index < MESH // 2, sample_index, sample_index - MESH).astype(
        jnp.float32
    )
    wavenumber = 2.0 * jnp.pi * signed
    squares = (
        wavenumber[:, None, None] ** 2
        + wavenumber[None, :, None] ** 2
        + wavenumber[None, None, :] ** 2
    )
    kappa_sq = screening[:, None, None, None] ** 2
    return (
        kappa_sq
        * jnp.exp(-0.5 * squares[None] * smearing[:, None, None, None] ** 2)
        / (squares[None] + kappa_sq)
    )


def smooth_field(field_grid, screening, smearing):
    sample_index = jnp.arange(MESH, dtype=jnp.int32)
    phase_index = sample_index[:, None] * sample_index[None, :] % MESH
    angle_grid = phase_index.astype(jnp.float32) * (2.0 * jnp.pi / MESH)
    table = (jnp.cos(angle_grid) + jnp.sin(angle_grid)) * (MESH**-0.5)
    grid = jnp.einsum("cuvw,wk->cuvk", field_grid, table, precision=fine)
    grid = jnp.einsum("cuvw,vk->cukw", grid, table, precision=fine)
    grid = jnp.einsum("cuvw,uk->ckvw", grid, table, precision=fine)
    grid = grid * filter_kernel(screening, smearing)
    grid = jnp.einsum("cuvw,uk->ckvw", grid, table, precision=fine)
    grid = jnp.einsum("cuvw,vk->cukw", grid, table, precision=fine)
    return jnp.einsum("cuvw,wk->cuvk", grid, table, precision=fine)


def on_device(
    features,
    positions,
    tile_lists,
    value_proj,
    radial_mix,
    charge_proj,
    screening,
    smearing,
    mesh_gain,
    mesh_up,
    mesh_down,
    long_proj,
    atom_gain,
    atom_up,
    atom_down,
):
    wide_count = lax.axis_size("wide")
    sixteen_count = lax.axis_size("sixteen")
    devices = wide_count * sixteen_count
    channels = charge_proj.shape[1]
    local_channels = screening.shape[0]
    slab_x = MESH // wide_count
    slab_y = MESH // sixteen_count
    slab_cells = slab_x * slab_y * MESH
    near_features, near_positions = (
        extended_2(features, (("wide", 0), ("sixteen", 1)), 1),
        extended_2(positions, (("wide", 0), ("sixteen", 1)), 1),
    )
    own_features = features[0, 0]
    own_pos = positions[0, 0]
    atoms = own_features.shape[0]
    per_plane = atoms // MESH
    weights = []
    sources = []
    for step_x, step_y in ((0, 0), (-1, 0), (0, -1), (-1, -1)):
        weights.append(
            plane_weights(
                near_positions[1 + step_x, 1 + step_y],
                step_x, step_y, slab_x, slab_y, slab_x, slab_y,
            )
        )
        charges = jnp.dot(
            near_features[1 + step_x, 1 + step_y], charge_proj, precision=fine
        ).reshape(MESH, per_plane, channels)
        sources.append(jnp.concatenate([charges, jnp.roll(charges, 1, axis=0)], axis=1))
    slab = jnp.einsum(
        "zac,zan->zcn",
        jnp.concatenate(sources, axis=1),
        jnp.concatenate(weights, axis=1),
        precision=fine,
    ).transpose(1, 0, 2)
    grouped = lax.all_to_all(
        slab.reshape(devices, local_channels, MESH, slab_x * slab_y),
        ("wide", "sixteen"),
        split_axis=0,
        concat_axis=0,
        tiled=True,
    )
    values = jnp.einsum("xyaf,fg->xyag", near_features, value_proj, precision=fine)
    messages = short_range(
        values, near_positions, tile_lists[0, 0], radial_mix, wide_count, sixteen_count
    )
    grouped = grouped.reshape(wide_count, sixteen_count, local_channels, MESH, slab_x, slab_y)
    field_grid = grouped.transpose(2, 3, 0, 4, 1, 5).reshape(local_channels, MESH, MESH, MESH)
    potential = smooth_field(field_grid, screening, smearing)
    outgoing = potential.reshape(
        local_channels, MESH, wide_count, slab_x, sixteen_count, slab_y
    ).transpose(2, 4, 0, 1, 3, 5)
    by_cells = lax.all_to_all(
        outgoing.reshape(devices, local_channels, MESH, slab_x * slab_y),
        ("wide", "sixteen"),
        split_axis=0,
        concat_axis=0,
        tiled=True,
    ).reshape(channels, slab_cells)
    inverse_rms = lax.rsqrt(jnp.mean(by_cells**2, axis=0, keepdims=True) + 1e-06)
    normed = by_cells * inverse_rms * mesh_gain[:, None]
    hidden = jax.nn.silu(jnp.einsum("cn,ch->nh", normed, mesh_up, precision=fine))
    mesh_out = jnp.dot(hidden, mesh_down, precision=fine).reshape(MESH, slab_x, slab_y, channels)
    face_x = passed_along(mesh_out[:, 0], "wide", -1)
    face_y = passed_along(
        jnp.concatenate([mesh_out[:, :, 0], face_x[:, :1]], axis=1), "sixteen", -1
    )
    corners = plane_weights(
        own_pos, 0, 0, slab_x, slab_y, slab_x + 1, slab_y + 1
    ).reshape(MESH, 2 * per_plane, slab_x + 1, slab_y + 1)
    gathered = jnp.einsum(
        "zan,znc->zac",
        corners[:, :, :slab_x, :slab_y].reshape(MESH, 2 * per_plane, slab_x * slab_y),
        mesh_out.reshape(MESH, slab_x * slab_y, channels),
        precision=fine,
    )
    gathered += jnp.einsum("zan,znc->zac", corners[:, :, slab_x, :slab_y], face_x, precision=fine)
    gathered += jnp.einsum("zan,znc->zac", corners[:, :, :, slab_y], face_y, precision=fine)
    at_atoms = gathered[:, :per_plane] + jnp.roll(gathered[:, per_plane:], -1, axis=0)
    long_terms = jnp.dot(at_atoms.reshape(atoms, channels), long_proj, precision=fine)
    summed = own_features + messages + long_terms
    inverse_rms = lax.rsqrt(jnp.mean(summed**2, axis=-1, keepdims=True) + 1e-06)
    normed = summed * inverse_rms * atom_gain
    hidden = jax.nn.silu(jnp.dot(normed, atom_up, precision=fine))
    updated = summed + jnp.dot(hidden, atom_down, precision=fine)
    return updated[None, None]


def solution(mesh):
    in_specs = (
        P("wide", "sixteen", None, None),
        P("wide", "sixteen", None, None),
        P("wide", "sixteen", None, None),
        P(),
        P(),
        P(),
        P(("wide", "sixteen")),
        P(("wide", "sixteen")),
        P(),
        P(),
        P(),
        P(),
        P(),
        P(),
        P(),
    )
    out_specs = P("wide", "sixteen", None, None)
    return jax.shard_map(
        on_device, mesh=mesh, in_specs=in_specs, out_specs=out_specs, check_vma=False
    )
```
